32 devices in a mesh: dp: 16 (over z, y, core), tensor: 2 (over x).
Axes of the slice: x: 2, y: 2, z: 4, core: 2. Of those that a mesh axis runs over, the one named last changes fastest.
Arguments:
- block_in: bfloat16 [16, 1024, 1024], P('dp', 'tensor'), may hold values from -50 to 50
- valid_count: int32 [16], P('dp'), may hold values from 512 to 1024, as said below
- vectors: float32 [14, 1024], P(None, ('dp', 'tensor')), may hold values from -2 to 2
- qkv_weight: bfloat16 [3, 1024, 1024], P(None, 'dp', 'tensor'), may hold values from -1.5 to 1.5
- out_weight: bfloat16 [1024, 1024], P('tensor', 'dp'), may hold values from -1.5 to 1.5
- up_weight: bfloat16 [1024, 4096], P('dp', 'tensor'), may hold values from -0.1875 to 0.1875
- down_weight: bfloat16 [4096, 1024], P('tensor', 'dp'), may hold values from -0.09375 to 0.09375
- cotangent: bfloat16 [16, 1024, 1024], P('dp', 'tensor'), may hold values from -6 to 6
Outputs:
- block_out: bfloat16 [16, 1024, 1024], P('dp', 'tensor')
- grad_input: float32 [16, 1024, 1024], P('dp', 'tensor')
- grad_vectors: float32 [14, 1024], P(None, ('dp', 'tensor'))
- grad_qkv: float32 [3, 1024, 1024], P(None, 'dp', 'tensor')
- grad_proj: float32 [1024, 1024], P('tensor', 'dp')
- grad_up: float32 [1024, 4096], P('dp', 'tensor')
- grad_down: float32 [4096, 1024], P('tensor', 'dp')
The draws below stay inside these ranges and needn't reach their ends.
Inputs may be any that keep to these rules, and one draw needn't show every extreme that they name: Keys from position valid_count on are masked in their image; some image has all 1024 tokens valid.
All inputs are finite; a program needn't handle non-finite values.
Results may differ from the reference program's by a relative error of at most 0.019.
Values may be sent and summed in bfloat16 or wider, within the bound.
A program may use at most 192 MiB of HBM per device.

```python
import math
import jax
import jax.numpy as jnp
from jax import lax

D = 1024
FF = 4096
HEAD = 64
SEQ = 1024
IMAGES = 16
NVEC = 14


def draw_block_in(key, part):
    first, second, third = jax.random.split(key, 3)
    base = jnp.clip(jax.random.normal(first, (IMAGES, SEQ, D), jnp.float32), -4.0, 4.0)
    columns = jnp.exp(jax.random.uniform(second, (1, 1, D), jnp.float32, 0.0, math.log(10.0)))
    rows = jnp.exp(jax.random.uniform(third, (IMAGES, SEQ, 1), jnp.float32, -0.7, 0.7))
    return (base * columns * rows * 0.5).astype(jnp.bfloat16)


def draw_valid_count(key, part):
    first, second = jax.random.split(key)
    counts = jax.random.randint(first, (IMAGES,), SEQ // 2, SEQ + 1)
    chosen = jax.random.randint(second, (), 0, IMAGES)
    return jnp.where(jnp.arange(IMAGES) == chosen, SEQ, counts).astype(jnp.int32)


def draw_vectors(key, part):
    first, second = jax.random.split(key)
    row_ids = jnp.arange(NVEC)[:, None]
    is_gain = (row_ids == 0) | (row_ids == 5) | (row_ids == 6) | (row_ids == 9)
    gains = jax.random.uniform(first, (NVEC, D), jnp.float32, 0.6, 1.5)
    shifts = 0.45 * jnp.clip(jax.random.normal(second, (NVEC, D), jnp.float32), -4.0, 4.0)
    return jnp.where(is_gain, gains, shifts)


def draw_qkv_weight(key, part):
    return (jnp.clip(jax.random.normal(key, (3, D, D), jnp.float32), -4.0, 4.0) * D ** (-0.5)).astype(jnp.bfloat16)


def shard_levels(key, shape, pieces, low, high):
    loudness = 1.0
    for axis_at, blocks in pieces:
        draws = jax.random.uniform(jax.random.fold_in(jax.random.fold_in(key, 6), axis_at), (blocks,), jnp.float32, low / len(pieces), high / len(pieces))
        loudness = loudness * jnp.repeat(jnp.exp(draws), shape[axis_at] // blocks).reshape((-1,) + (1,) * (len(shape) - 1 - axis_at))
    return loudness


def gaussian(own_key, dims, width, most, cuts=(), held_as=jnp.bfloat16):
    values = width * jax.random.normal(own_key, dims, jnp.float32)
    if cuts:
        values = values * shard_levels(own_key, dims, cuts, -0.22, 0.18)
    return jnp.clip(values, -most, most).astype(held_as)


def setup_inputs(seed: int = 0) -> dict:
    key_list = jax.random.split(jax.random.key(seed), 9)
    return {
        "block_in": draw_block_in(jax.random.fold_in(key_list[8], 71), 0),
        "valid_count": draw_valid_count(jax.random.fold_in(key_list[8], 71), 0),
        "vectors": draw_vectors(jax.random.fold_in(key_list[8], 71), 0),
        "qkv_weight": draw_qkv_weight(jax.random.fold_in(key_list[8], 71), 0),
        "out_weight": gaussian(key_list[4], (D, D), (D * 16 // SEQ) ** -0.5, 1.5, ((0, 2), (1, 16))),
        "up_weight": gaussian(key_list[5], (D, FF), D ** -0.5, 0.1875, ((0, 16), (1, 2))),
        "down_weight": gaussian(key_list[6], (FF, D), FF ** -0.5, 0.09375, ((0, 2), (1, 16))),
        "cotangent": gaussian(key_list[7], (IMAGES, SEQ, D), 1.0, 6.0, ((0, 16), (1, 2))),
    }


NORM_EPS = 1e-06
ROOT_HALF = 0.7071067811865476
INV_ROOT_TAU = 0.3989422804014327
MASKED = -1e+30

def to_low(values):
    return lax.optimization_barrier(values.astype(jnp.bfloat16))

def layer_norm(values):
    center = values - lax.optimization_barrier(jnp.mean(values, axis=-1, keepdims=True))
    inverse = lax.rsqrt(lax.optimization_barrier(jnp.mean(center * center, axis=-1, keepdims=True)) + NORM_EPS)
    return (center * inverse, inverse)

def norm_back(grad_hat, normed, inverse):
    first_mean = lax.optimization_barrier(jnp.mean(grad_hat, axis=-1, keepdims=True))
    second_mean = lax.optimization_barrier(jnp.mean(grad_hat * normed, axis=-1, keepdims=True))
    return inverse * (grad_hat - first_mean - normed * second_mean)

def gelu_pair(hidden):
    cumul = 0.5 * (1.0 + jax.scipy.special.erf(hidden * ROOT_HALF))
    density = jnp.exp(-0.5 * hidden * hidden) * INV_ROOT_TAU
    return (hidden * cumul, cumul + hidden * density)

def matmul(left_side, right_side):
    return jnp.dot(left_side, right_side, preferred_element_type=jnp.float32)

def masked_scores(queries, key_rows, visible, score_scale):
    scores = jnp.einsum('qhe,khe->hqk', queries.astype(jnp.float32), key_rows.astype(jnp.float32)) * score_scale
    return jnp.where(visible[None, None, :], scores, MASKED)

def attend(queries, key_rows, value_rows, visible, score_scale):
    scores = masked_scores(queries, key_rows, visible, score_scale)
    row_max = lax.optimization_barrier(jnp.max(scores, axis=-1, keepdims=True))
    log_total = row_max + jnp.log(lax.optimization_barrier(jnp.sum(jnp.exp(scores - row_max), axis=-1, keepdims=True)))
    weights_low = to_low(jnp.exp(scores - log_total))
    mixed = jnp.einsum('hqk,khe->qhe', weights_low.astype(jnp.float32), value_rows.astype(jnp.float32))
    return (to_low(mixed), log_total)

def attend_back(queries, key_rows, value_rows, mixed, grad_mixed, log_total, visible, score_scale):
    probs = jnp.exp(masked_scores(queries, key_rows, visible, score_scale) - log_total)
    probs_low = to_low(probs)
    grad_wide = grad_mixed.astype(jnp.float32)
    grad_values = jnp.einsum('hqk,qhe->khe', probs_low.astype(jnp.float32), grad_wide)
    grad_probs = jnp.einsum('qhe,khe->hqk', grad_wide, value_rows.astype(jnp.float32))
    delta = jnp.einsum('qhe,qhe->hq', grad_wide, mixed.astype(jnp.float32))[:, :, None]
    grad_scores = to_low(probs * (grad_probs - delta)).astype(jnp.float32)
    grad_queries = score_scale * jnp.einsum('hqk,khe->qhe', grad_scores, key_rows.astype(jnp.float32))
    grad_keys = score_scale * jnp.einsum('hqk,qhe->khe', grad_scores, queries.astype(jnp.float32))
    return (grad_queries, grad_keys, grad_values)

def one_image(image_in, image_valid, image_cot, vectors, qkv_weight, out_weight, up_weight, down_weight):
    seq_len, model_width = image_in.shape
    head_count = model_width // HEAD
    score_scale = HEAD ** (-0.5)
    gain_one, shift_one, bias_query, bias_value, bias_out, scale_one, gain_two, shift_two, bias_down, scale_two = vectors[:10]
    bias_up = vectors[10:].reshape(-1)
    input_rows = image_in.astype(jnp.float32)
    normed_one, inverse_one = layer_norm(input_rows)
    hidden_one = to_low(normed_one * gain_one + shift_one)
    queries = to_low(matmul(hidden_one, qkv_weight[0]) + bias_query).reshape(seq_len, head_count, HEAD)
    key_rows = to_low(matmul(hidden_one, qkv_weight[1])).reshape(seq_len, head_count, HEAD)
    value_rows = to_low(matmul(hidden_one, qkv_weight[2]) + bias_value).reshape(seq_len, head_count, HEAD)
    visible = jnp.arange(seq_len, dtype=jnp.int32) < image_valid
    mixed, log_total = attend(queries, key_rows, value_rows, visible, score_scale)
    mixed_flat = mixed.reshape(seq_len, model_width)
    branch_one = matmul(mixed_flat, out_weight) + bias_out
    middle = input_rows + scale_one * branch_one
    normed_two, inverse_two = layer_norm(middle)
    hidden_two = to_low(normed_two * gain_two + shift_two)
    activated, gelu_slope = gelu_pair(matmul(hidden_two, up_weight) + bias_up)
    act_low = to_low(activated)
    branch_two = matmul(act_low, down_weight) + bias_down
    block_out = (middle + scale_two * branch_two).astype(jnp.bfloat16)
    grad_rows = image_cot.astype(jnp.float32)
    grad_scale_two = lax.optimization_barrier(jnp.sum(grad_rows * branch_two, axis=0))
    grad_bias_down = lax.optimization_barrier(jnp.sum(grad_rows * scale_two, axis=0))
    grad_branch_two = to_low(grad_rows * scale_two)
    grad_down = matmul(act_low.T, grad_branch_two)
    grad_pre = matmul(grad_branch_two, down_weight.T) * gelu_slope
    grad_bias_up = lax.optimization_barrier(jnp.sum(grad_pre, axis=0))
    grad_pre_low = to_low(grad_pre)
    grad_up = matmul(hidden_two.T, grad_pre_low)
    grad_hidden_two = matmul(grad_pre_low, up_weight.T)
    grad_gain_two = lax.optimization_barrier(jnp.sum(grad_hidden_two * normed_two, axis=0))
    grad_shift_two = lax.optimization_barrier(jnp.sum(grad_hidden_two, axis=0))
    grad_middle = grad_rows + norm_back(grad_hidden_two * gain_two, normed_two, inverse_two)
    grad_scale_one = lax.optimization_barrier(jnp.sum(grad_middle * branch_one, axis=0))
    grad_bias_out = lax.optimization_barrier(jnp.sum(grad_middle * scale_one, axis=0))
    grad_branch_one = to_low(grad_middle * scale_one)
    grad_proj = matmul(mixed_flat.T, grad_branch_one)
    grad_mixed = to_low(matmul(grad_branch_one, out_weight.T)).reshape(seq_len, head_count, HEAD)
    grad_queries, grad_keys, grad_values = attend_back(queries, key_rows, value_rows, mixed, grad_mixed, log_total, visible, score_scale)
    grad_queries = grad_queries.reshape(seq_len, model_width)
    grad_keys = grad_keys.reshape(seq_len, model_width)
    grad_values = grad_values.reshape(seq_len, model_width)
    grad_bias_query = lax.optimization_barrier(jnp.sum(grad_queries, axis=0))
    grad_bias_value = lax.optimization_barrier(jnp.sum(grad_values, axis=0))
    query_low = to_low(grad_queries)
    key_low = to_low(grad_keys)
    value_low = to_low(grad_values)
    grad_qkv = jnp.stack([matmul(hidden_one.T, query_low), matmul(hidden_one.T, key_low), matmul(hidden_one.T, value_low)])
    grad_hidden_one = matmul(query_low, qkv_weight[0].T) + matmul(key_low, qkv_weight[1].T) + matmul(value_low, qkv_weight[2].T)
    grad_gain_one = lax.optimization_barrier(jnp.sum(grad_hidden_one * normed_one, axis=0))
    grad_shift_one = lax.optimization_barrier(jnp.sum(grad_hidden_one, axis=0))
    grad_input = grad_middle + norm_back(grad_hidden_one * gain_one, normed_one, inverse_one)
    grad_vectors = jnp.concatenate([jnp.stack([grad_gain_one, grad_shift_one, grad_bias_query, grad_bias_value, grad_bias_out, grad_scale_one, grad_gain_two, grad_shift_two, grad_bias_down, grad_scale_two]), grad_bias_up.reshape(-1, model_width)], axis=0)
    return (block_out, grad_input, (grad_vectors, grad_qkv, grad_proj, grad_up, grad_down))

def reference(block_in, valid_count, vectors, qkv_weight, out_weight, up_weight, down_weight, cotangent):

    def step_image(carry, item):
        image_in, image_valid, image_cot = item
        out_rows, grad_rows, grads = one_image(image_in, image_valid, image_cot, vectors, qkv_weight, out_weight, up_weight, down_weight)
        return (tuple((running + addend for running, addend in zip(carry, grads))), (out_rows, grad_rows))
    start_carry = (jnp.zeros(vectors.shape, jnp.float32), jnp.zeros(qkv_weight.shape, jnp.float32), jnp.zeros(out_weight.shape, jnp.float32), jnp.zeros(up_weight.shape, jnp.float32), jnp.zeros(down_weight.shape, jnp.float32))
    carry, (block_out, grad_input) = lax.scan(step_image, start_carry, (block_in, valid_count, cotangent))
    return (block_out, grad_input, carry[0], carry[1], carry[2], carry[3], carry[4])
```

```python
import jax
import jax.numpy as jnp
from jax import lax
from jax.sharding import PartitionSpec as P

HEAD = 64
NORM_EPS = 1e-06
ROOT_HALF = 0.7071067811865476
INV_ROOT_TAU = 0.3989422804014327
MASKED = -1e30
F32 = jnp.float32
BF16 = jnp.bfloat16


def layer_norm(values):
    center = values - jnp.mean(values, axis=-1, keepdims=True)
    inverse = lax.rsqrt(jnp.mean(center * center, axis=-1, keepdims=True) + NORM_EPS)
    return (center * inverse, inverse)


def norm_back(grad_hat, normed, inverse):
    first_mean = jnp.mean(grad_hat, axis=-1, keepdims=True)
    second_mean = jnp.mean(grad_hat * normed, axis=-1, keepdims=True)
    return inverse * (grad_hat - first_mean - normed * second_mean)


def gelu_pair(hidden):
    cumul = 0.5 * (1.0 + jax.scipy.special.erf(hidden * ROOT_HALF))
    density = jnp.exp(-0.5 * hidden * hidden) * INV_ROOT_TAU
    return (hidden * cumul, cumul + hidden * density)


def mm(a, b):
    return jnp.dot(a, b, preferred_element_type=F32)


def mm_nt(a, b):
    return lax.dot_general(a, b, (((1,), (1,)), ((), ())), preferred_element_type=F32)


def mm_tn(a, b):
    return lax.dot_general(a, b, (((0,), (0,)), ((), ())), preferred_element_type=F32)


def swap(x, axis, stride):
    n = lax.axis_size(axis)
    return lax.ppermute(x, axis, [(i, i ^ stride) for i in range(n)])


def bit_of(axis, stride):
    return (lax.axis_index(axis) // stride) % 2


def gather_step(cur, axis, stride):
    other = swap(cur, axis, stride)
    high = bit_of(axis, stride) == 1
    pair = jnp.stack([jnp.where(high, other, cur), jnp.where(high, cur, other)], axis=1)
    return pair.reshape((2 * cur.shape[0],) + cur.shape[1:])


def scatter_step(cur, axis, stride):
    pair = cur.reshape((cur.shape[0] // 2, 2) + cur.shape[1:])
    mine = bit_of(axis, stride)
    send = lax.dynamic_index_in_dim(pair, 1 - mine, axis=1, keepdims=False)
    keep = lax.dynamic_index_in_dim(pair, mine, axis=1, keepdims=False)
    return keep, swap(send, axis, stride)


def strides_of(axis):
    n = lax.axis_size(axis)
    out = []
    s = 1
    while s < n:
        out.append(s)
        s *= 2
    return out


def gather_rows(shard, after=None):
    if after is not None:
        shard, _ = lax.optimization_barrier((shard, after))
    cur = shard[None]
    marks = []
    for stride in reversed(strides_of("dp")):
        cur = gather_step(cur, "dp", stride)
        marks.append(cur)
    return cur.reshape((-1,) + shard.shape[1:]), marks


def scatter_rows(grad):
    n = lax.axis_size("dp")
    cur = grad.reshape((n, grad.shape[0] // n) + grad.shape[1:]).astype(BF16)
    total = None
    for stride in strides_of("dp"):
        keep, got = scatter_step(cur, "dp", stride)
        total = keep.astype(F32) + got.astype(F32)
        cur = total.astype(BF16)
    return total[0]


def local(
    block_in, valid_count, vectors, qkv_weight, out_weight, up_weight, down_weight, cotangent
):
    rank = lax.axis_index("tensor")
    half = block_in.shape[1]
    ways = lax.axis_size("tensor")
    rest = (ways - 1) * half
    seq_len = ways * half
    width = qkv_weight.shape[2]
    heads = width // HEAD
    units = up_weight.shape[1]
    scale = HEAD ** (-0.5)

    def from_others(x):
        return jnp.concatenate([swap(x, "tensor", j) for j in range(1, ways)], axis=0)

    def sum_to_owner(parts):
        total = None
        for j in range(1, ways):
            got = swap(parts[(j - 1) * half : j * half], "tensor", j).astype(F32)
            total = got if total is None else total + got
        return total

    x_own_low = block_in[0]
    x_oth_low = from_others(x_own_low)
    c_own_low = cotangent[0]

    cur = vectors[None]
    for stride in reversed(strides_of("dp")):
        cur = gather_step(cur, "dp", stride)
    for stride in reversed(strides_of("tensor")):
        cur = gather_step(cur, "tensor", stride)
    params = jnp.transpose(cur, (1, 0, 2)).reshape(vectors.shape[0], -1)
    model = params.shape[1]

    qkv_rows = jnp.transpose(qkv_weight, (1, 0, 2)).reshape(qkv_weight.shape[1], -1)
    w_qkv, marks_a = gather_rows(qkv_rows)
    w_out, marks_b = gather_rows(out_weight.T, marks_a[-3][0, 0, 0])
    w_up, marks_c = gather_rows(up_weight, marks_b[-3][0, 0, 0])
    w_down, _ = gather_rows(down_weight.T, marks_c[-3][0, 0, 0])
    c_own_low, _ = lax.optimization_barrier((c_own_low, x_oth_low[0, 0]))
    c_oth_low = from_others(c_own_low)

    g1, s1, bq_all, bv_all, bo, l1, g2, s2, bd, l2 = params[:10]
    b_query = lax.dynamic_slice_in_dim(bq_all, rank * width, width)
    b_value = lax.dynamic_slice_in_dim(bv_all, rank * width, width)
    b_up = lax.dynamic_slice_in_dim(params[10:].reshape(-1), rank * units, units)

    x_own = x_own_low.astype(F32)
    n1_own, r1 = layer_norm(x_own)
    n1_oth, _ = layer_norm(x_oth_low.astype(F32))
    h1 = jnp.concatenate(
        [(n1_own * g1 + s1).astype(BF16), (n1_oth * g1 + s1).astype(BF16)], axis=0
    )
    bias = jnp.concatenate([b_query, jnp.zeros_like(b_query), b_value])
    qkv = (mm(h1, w_qkv) + bias).astype(BF16)
    keys = qkv[:, width : 2 * width].reshape(seq_len, heads, HEAD)
    values = qkv[:, 2 * width :].reshape(seq_len, heads, HEAD)
    order = lax.iota(jnp.int32, half)
    positions = jnp.concatenate([(rank ^ j) * half + order for j in range(ways)])
    visible = (positions < valid_count[0])[None, None, :]

    def scores_of(q):
        s = jnp.einsum("qhe,khe->hqk", q, keys, preferred_element_type=F32) * scale
        return jnp.where(visible, s, MASKED)

    def attend(q):
        s = scores_of(q)
        top = jnp.max(s, axis=-1, keepdims=True)
        lse = top + jnp.log(jnp.sum(jnp.exp(s - top), axis=-1, keepdims=True))
        p = jnp.exp(s - lse).astype(BF16)
        o = jnp.einsum("hqk,khe->qhe", p, values, preferred_element_type=F32)
        return o.astype(BF16), lse

    def attend_back(q, o, do, lse):
        pf = jnp.exp(scores_of(q) - lse)
        dv = jnp.einsum("hqk,qhe->khe", pf.astype(BF16), do, preferred_element_type=F32)
        dp = jnp.einsum("qhe,khe->hqk", do, values, preferred_element_type=F32)
        delta = jnp.einsum("qhe,qhe->hq", do, o, preferred_element_type=F32)[:, :, None]
        ds = (pf * (dp - delta)).astype(BF16)
        dq = scale * jnp.einsum("hqk,khe->qhe", ds, keys, preferred_element_type=F32)
        dk = scale * jnp.einsum("hqk,qhe->khe", ds, q, preferred_element_type=F32)
        return (
            dq.reshape(-1, width),
            dk.reshape(seq_len, width),
            dv.reshape(seq_len, width),
        )

    q_own = qkv[:half, :width].reshape(half, heads, HEAD)
    q_oth = qkv[half:, :width].reshape(rest, heads, HEAD)
    o_oth, lse_oth = attend(q_oth)
    got = sum_to_owner(mm_nt(o_oth.reshape(rest, width), w_out).astype(BF16))
    q_own, _ = lax.optimization_barrier((q_own, o_oth[0, 0, 0]))
    o_own, lse_own = attend(q_own)
    branch_one = mm_nt(o_own.reshape(half, width), w_out) + got + bo
    o_flat = jnp.concatenate([o_own.reshape(half, width), o_oth.reshape(rest, width)], axis=0)

    y1 = x_own + l1 * branch_one
    n2, r2 = layer_norm(y1)
    h2_own = (n2 * g2 + s2).astype(BF16)
    h2_oth = from_others(h2_own)
    c_own = c_own_low.astype(F32)
    dm_own = (c_own * l2).astype(BF16)
    dm_oth = (c_oth_low.astype(F32) * l2).astype(BF16)

    def feed(h2, dm):
        act, slope = gelu_pair(mm(h2, w_up) + b_up)
        du = mm(dm, w_down) * slope
        return act.astype(BF16), du.astype(BF16), jnp.sum(du, axis=0)

    act_own, du_own, dbu_own = feed(h2_own, dm_own)
    act_oth, du_oth, dbu_oth = feed(h2_oth, dm_oth)
    got_dh2 = sum_to_owner(mm_nt(du_oth, w_up).astype(BF16))
    dh2 = mm_nt(du_own, w_up) + got_dh2
    m_send = mm_nt(act_oth, w_down).astype(BF16)
    m_send, _ = lax.optimization_barrier((m_send, got_dh2[0, 0]))
    got_m = sum_to_owner(m_send)
    branch_two = mm_nt(act_own, w_down) + got_m + bd
    block_out = (y1 + l2 * branch_two).astype(BF16)
    d_l2 = jnp.sum(c_own * branch_two, axis=0)
    d_bd = jnp.sum(c_own * l2, axis=0)
    d_bu = dbu_own + dbu_oth
    du = jnp.concatenate([du_own, du_oth], axis=0)
    act = jnp.concatenate([act_own, act_oth], axis=0)
    h2 = jnp.concatenate([h2_own, h2_oth], axis=0)
    dm = jnp.concatenate([dm_own, dm_oth], axis=0)
    owned_down = scatter_rows(mm_tn(dm, act)).T
    owned_up = scatter_rows(mm_tn(h2, du))

    d_g2 = jnp.sum(dh2 * n2, axis=0)
    d_s2 = jnp.sum(dh2, axis=0)
    dy1 = c_own + norm_back(dh2 * g2, n2, r2)
    d_l1 = jnp.sum(dy1 * branch_one, axis=0)
    d_bo = jnp.sum(dy1 * l1, axis=0)

    da_own = (dy1 * l1).astype(BF16)
    da_oth = from_others(da_own)
    do_own = mm(da_own, w_out).astype(BF16).reshape(half, heads, HEAD)
    dq_own, dk_one, dv_one = attend_back(q_own, o_own, do_own, lse_own)
    do_oth = mm(da_oth, w_out).astype(BF16).reshape(rest, heads, HEAD)
    dq_oth, dk_two, dv_two = attend_back(q_oth, o_oth, do_oth, lse_oth)
    da = jnp.concatenate([da_own, da_oth], axis=0)
    owned_proj = scatter_rows(mm_tn(da, o_flat)).T
    dq = jnp.concatenate([dq_own, dq_oth], axis=0)
    dk = dk_one + dk_two
    dv = dv_one + dv_two
    d_bq = jnp.sum(dq, axis=0)
    d_bv = jnp.sum(dv, axis=0)
    dqkv = jnp.concatenate([dq.astype(BF16), dk.astype(BF16), dv.astype(BF16)], axis=1)
    got_dh1 = sum_to_owner(mm_nt(dqkv[half:], w_qkv).astype(BF16))
    dh1 = mm_nt(dqkv[:half], w_qkv) + got_dh1
    owned_rows = scatter_rows(mm_tn(h1, dqkv))
    owned_qkv = jnp.transpose(owned_rows.reshape(-1, 3, width), (1, 0, 2))
    d_g1 = jnp.sum(dh1 * n1_own, axis=0)
    d_s1 = jnp.sum(dh1, axis=0)
    grad_input = dy1 + norm_back(dh1 * g1, n1_own, r1)

    zero_row = jnp.zeros((model,), F32)
    placed_query = lax.dynamic_update_slice_in_dim(zero_row, d_bq, rank * width, 0)
    placed_value = lax.dynamic_update_slice_in_dim(zero_row, d_bv, rank * width, 0)
    placed_up = lax.dynamic_update_slice_in_dim(
        jnp.zeros((params[10:].size,), F32), d_bu, rank * units, 0
    )
    image_params = jnp.concatenate(
        [
            jnp.stack(
                [d_g1, d_s1, placed_query, placed_value, d_bo, d_l1, d_g2, d_s2, d_bd, d_l2]
            ),
            placed_up.reshape(-1, model),
        ],
        axis=0,
    )
    rows, cols = vectors.shape
    cur = jnp.transpose(image_params.reshape(rows, model // cols, cols), (1, 0, 2))
    for stride in strides_of("tensor"):
        keep, got_p = scatter_step(cur, "tensor", stride)
        cur = keep + got_p
    for stride in strides_of("dp"):
        keep, got_p = scatter_step(cur, "dp", stride)
        cur = keep + got_p
    return (
        block_out[None],
        grad_input[None],
        cur[0],
        owned_qkv,
        owned_proj,
        owned_up,
        owned_down,
    )


def solution(mesh):
    placed = (
        P("dp", "tensor", None),
        P("dp"),
        P(None, ("dp", "tensor")),
        P(None, "dp", "tensor"),
        P("tensor", "dp"),
        P("dp", "tensor"),
        P("tensor", "dp"),
        P("dp", "tensor", None),
    )
    return jax.shard_map(
        local,
        mesh=mesh,
        in_specs=placed,
        out_specs=(
            P("dp", "tensor", None),
            P("dp", "tensor", None),
            P(None, ("dp", "tensor")),
            P(None, "dp", "tensor"),
            P("tensor", "dp"),
            P("dp", "tensor"),
            P("tensor", "dp"),
        ),
        check_vma=False,
    )
```

```python
import jax
import jax.numpy as jnp
from jax import lax
from jax.sharding import PartitionSpec as P

HEAD = 64
NORM_EPS = 1e-06
ROOT_HALF = 0.7071067811865476
INV_ROOT_TAU = 0.3989422804014327
MASKED = -1e30
F32 = jnp.float32
BF16 = jnp.bfloat16


def layer_norm(values):
    center = values - jnp.mean(values, axis=-1, keepdims=True)
    inverse = lax.rsqrt(jnp.mean(center * center, axis=-1, keepdims=True) + NORM_EPS)
    return (center * inverse, inverse)


def norm_back(grad_hat, normed, inverse):
    first_mean = jnp.mean(grad_hat, axis=-1, keepdims=True)
    second_mean = jnp.mean(grad_hat * normed, axis=-1, keepdims=True)
    return inverse * (grad_hat - first_mean - normed * second_mean)


def gelu_pair(hidden):
    cumul = 0.5 * (1.0 + jax.scipy.special.erf(hidden * ROOT_HALF))
    density = jnp.exp(-0.5 * hidden * hidden) * INV_ROOT_TAU
    return (hidden * cumul, cumul + hidden * density)


def mm(a, b):
    return jnp.dot(a, b, preferred_element_type=F32)


def mm_nt(a, b):
    return lax.dot_general(a, b, (((1,), (1,)), ((), ())), preferred_element_type=F32)


def mm_tn(a, b):
    return lax.dot_general(a, b, (((0,), (0,)), ((), ())), preferred_element_type=F32)


def swap(x, axis, stride):
    n = lax.axis_size(axis)
    return lax.ppermute(x, axis, [(i, i ^ stride) for i in range(n)])


def bit_of(axis, stride):
    return (lax.axis_index(axis) // stride) % 2


def gather_step(cur, axis, stride):
    other = swap(cur, axis, stride)
    high = bit_of(axis, stride) == 1
    pair = jnp.stack([jnp.where(high, other, cur), jnp.where(high, cur, other)], axis=1)
    return pair.reshape((2 * cur.shape[0],) + cur.shape[1:])


def scatter_step(cur, axis, stride):
    pair = cur.reshape((cur.shape[0] // 2, 2) + cur.shape[1:])
    mine = bit_of(axis, stride)
    send = lax.dynamic_index_in_dim(pair, 1 - mine, axis=1, keepdims=False)
    keep = lax.dynamic_index_in_dim(pair, mine, axis=1, keepdims=False)
    return keep, swap(send, axis, stride)


def strides_of(axis):
    n = lax.axis_size(axis)
    out = []
    s = 1
    while s < n:
        out.append(s)
        s *= 2
    return out


def gather_rows(shard, mark):
    cur = after(shard, mark)[None]
    marks = []
    for stride in reversed(strides_of("dp")):
        cur = gather_step(cur, "dp", stride)
        marks.append(cur)
    return cur.reshape((-1,) + shard.shape[1:]), marks


def scatter_rows(grad):
    n = lax.axis_size("dp")
    cur = grad.reshape((n, grad.shape[0] // n) + grad.shape[1:]).astype(BF16)
    total = None
    marks = []
    for stride in strides_of("dp"):
        keep, got = scatter_step(cur, "dp", stride)
        total = keep.astype(F32) + got.astype(F32)
        cur = total.astype(BF16)
        marks.append(cur[0, 0, 0])
    return total[0], marks


def after(value, *others):
    zero = sum(o.astype(F32) * 0.0 for o in others)
    return value + zero.astype(value.dtype)


def local(
    block_in, valid_count, vectors, qkv_weight, out_weight, up_weight, down_weight, cotangent
):
    rank = lax.axis_index("tensor")
    half = block_in.shape[1]
    ways = lax.axis_size("tensor")
    rest = (ways - 1) * half
    seq_len = ways * half
    width = qkv_weight.shape[2]
    heads = width // HEAD
    units = up_weight.shape[1]
    scale = HEAD ** (-0.5)

    def from_others(x):
        return jnp.concatenate([swap(x, "tensor", j) for j in range(1, ways)], axis=0)

    def sum_to_owner(parts):
        total = None
        for j in range(1, ways):
            got = swap(parts[(j - 1) * half : j * half], "tensor", j).astype(F32)
            total = got if total is None else total + got
        return total

    x_own_low = block_in[0]
    c_own_low = cotangent[0]

    cur = vectors[None]
    for stride in reversed(strides_of("tensor")):
        cur = gather_step(cur, "tensor", stride)
    x_oth_low = from_others(after(x_own_low, cur[0, 0, 0]))
    qkv_rows = jnp.transpose(qkv_weight, (1, 0, 2)).reshape(qkv_weight.shape[1], -1)
    cur_w = qkv_rows[None]
    cur = cur[None]
    marks_a = []
    for stride in reversed(strides_of("dp")):
        cur = gather_step(cur, "dp", stride)
        cur_w = gather_step(cur_w, "dp", stride)
        cur = after(cur, cur_w[0, 0, 0])
        marks_a.append(cur_w)
    w_qkv = cur_w.reshape(-1, qkv_rows.shape[1])
    params = jnp.transpose(cur, (2, 0, 1, 3)).reshape(vectors.shape[0], -1)
    model = params.shape[1]

    w_out, marks_b = gather_rows(out_weight.T, marks_a[-3][0, 0, 0])
    w_up, marks_c = gather_rows(up_weight, marks_b[-3][0, 0, 0])
    w_down, _ = gather_rows(down_weight.T, marks_c[-3][0, 0, 0])
    c_own_low = after(c_own_low, w_qkv[0, 0])
    c_oth_low = from_others(c_own_low)

    g1, s1, bq_all, bv_all, bo, l1, g2, s2, bd, l2 = params[:10]
    b_query = lax.dynamic_slice_in_dim(bq_all, rank * width, width)
    b_value = lax.dynamic_slice_in_dim(bv_all, rank * width, width)
    b_up = lax.dynamic_slice_in_dim(params[10:].reshape(-1), rank * units, units)

    x_own = x_own_low.astype(F32)
    n1_own, r1 = layer_norm(x_own)
    n1_oth, _ = layer_norm(x_oth_low.astype(F32))
    h1 = jnp.concatenate(
        [(n1_own * g1 + s1).astype(BF16), (n1_oth * g1 + s1).astype(BF16)], axis=0
    )
    bias = jnp.concatenate([b_query, jnp.zeros_like(b_query), b_value])
    qkv = (mm(h1, w_qkv) + bias).astype(BF16)
    keys = qkv[:, width : 2 * width].reshape(seq_len, heads, HEAD)
    values = qkv[:, 2 * width :].reshape(seq_len, heads, HEAD)
    order = lax.iota(jnp.int32, half)
    positions = jnp.concatenate([(rank ^ j) * half + order for j in range(ways)])
    visible = (positions < valid_count[0])[None, None, :]

    def scores_of(q):
        s = jnp.einsum("qhe,khe->hqk", q, keys, preferred_element_type=F32) * scale
        return jnp.where(visible, s, MASKED)

    def attend(q):
        s = scores_of(q)
        top = jnp.max(s, axis=-1, keepdims=True)
        lse = top + jnp.log(jnp.sum(jnp.exp(s - top), axis=-1, keepdims=True))
        p = jnp.exp(s - lse).astype(BF16)
        o = jnp.einsum("hqk,khe->qhe", p, values, preferred_element_type=F32)
        return o.astype(BF16), lse

    def attend_back(q, o, do, lse):
        pf = jnp.exp(scores_of(q) - lse)
        dv = jnp.einsum("hqk,qhe->khe", pf.astype(BF16), do, preferred_element_type=F32)
        dp = jnp.einsum("qhe,khe->hqk", do, values, preferred_element_type=F32)
        delta = jnp.einsum("qhe,qhe->hq", do, o, preferred_element_type=F32)[:, :, None]
        ds = (pf * (dp - delta)).astype(BF16)
        dq = scale * jnp.einsum("hqk,khe->qhe", ds, keys, preferred_element_type=F32)
        dk = scale * jnp.einsum("hqk,qhe->khe", ds, q, preferred_element_type=F32)
        return (
            dq.reshape(-1, width),
            dk.reshape(seq_len, width),
            dv.reshape(seq_len, width),
        )

    q_own = qkv[:half, :width].reshape(half, heads, HEAD)
    q_oth = qkv[half:, :width].reshape(rest, heads, HEAD)
    o_oth, lse_oth = attend(q_oth)
    got = sum_to_owner(mm_nt(o_oth.reshape(rest, width), w_out).astype(BF16))
    q_own = after(q_own, o_oth[0, 0, 0])
    o_own, lse_own = attend(q_own)
    branch_one = mm_nt(o_own.reshape(half, width), w_out) + got + bo
    o_flat = jnp.concatenate([o_own.reshape(half, width), o_oth.reshape(rest, width)], axis=0)

    y1 = x_own + l1 * branch_one
    n2, r2 = layer_norm(y1)
    h2_own = (n2 * g2 + s2).astype(BF16)
    h2_oth = from_others(h2_own)
    c_own = c_own_low.astype(F32)
    dm_own = (c_own * l2).astype(BF16)
    dm_oth = (c_oth_low.astype(F32) * l2).astype(BF16)

    def feed(h2, dm):
        act, slope = gelu_pair(mm(h2, w_up) + b_up)
        du = mm(dm, w_down) * slope
        return act.astype(BF16), du.astype(BF16), jnp.sum(du, axis=0)

    act_own, du_own, dbu_own = feed(h2_own, dm_own)
    act_oth, du_oth, dbu_oth = feed(h2_oth, dm_oth)
    send_dh2 = mm_nt(du_oth, w_up).astype(BF16)
    got_dh2 = sum_to_owner(send_dh2)
    dh2 = mm_nt(du_own, w_up) + got_dh2
    d_bd = jnp.sum(c_own * l2, axis=0)
    d_bu = dbu_own + dbu_oth
    du = jnp.concatenate([du_own, du_oth], axis=0)
    act = jnp.concatenate([act_own, act_oth], axis=0)
    h2 = jnp.concatenate([h2_own, h2_oth], axis=0)
    dm = jnp.concatenate([dm_own, dm_oth], axis=0)
    grad_down = mm_tn(after(dm, send_dh2[0, 0]), act).astype(BF16)
    grad_up = mm_tn(after(h2, send_dh2[0, 0]), du).astype(BF16)
    owned_down, mark_down = scatter_rows(grad_down)
    owned_up, mark_up = scatter_rows(grad_up)

    d_g2 = jnp.sum(dh2 * n2, axis=0)
    d_s2 = jnp.sum(dh2, axis=0)
    dy1 = c_own + norm_back(dh2 * g2, n2, r2)
    d_l1 = jnp.sum(dy1 * branch_one, axis=0)
    d_bo = jnp.sum(dy1 * l1, axis=0)

    da_own = (dy1 * l1).astype(BF16)
    da_oth = from_others(da_own)
    m_send = after(mm_nt(act_oth, w_down).astype(BF16), da_oth[0, 0])
    got_m = sum_to_owner(m_send)
    branch_two = mm_nt(act_own, w_down) + got_m + bd
    block_out = (y1 + l2 * branch_two).astype(BF16)
    d_l2 = jnp.sum(c_own * branch_two, axis=0)
    do_own = mm(da_own, w_out).astype(BF16).reshape(half, heads, HEAD)
    do_own = after(do_own, mark_down[0], mark_up[0])
    dq_own, dk_one, dv_one = attend_back(q_own, o_own, do_own, lse_own)
    do_oth = mm(da_oth, w_out).astype(BF16).reshape(rest, heads, HEAD)
    da = jnp.concatenate([da_own, da_oth], axis=0)
    grad_proj = mm_tn(da, o_flat).astype(BF16)
    do_oth = after(do_oth, dq_own[0, 0], grad_proj[0, 0], mark_down[1], mark_up[1])
    owned_proj, mark_proj = scatter_rows(grad_proj)
    dq_oth, dk_two, dv_two = attend_back(q_oth, o_oth, do_oth, lse_oth)
    dq = jnp.concatenate([dq_own, dq_oth], axis=0)
    dk = dk_one + dk_two
    dv = dv_one + dv_two
    d_bq = jnp.sum(dq, axis=0)
    d_bv = jnp.sum(dv, axis=0)
    dqkv = jnp.concatenate([dq.astype(BF16), dk.astype(BF16), dv.astype(BF16)], axis=1)
    dqkv = after(dqkv, mark_down[2], mark_up[2], mark_proj[0], got_m[0, 0])
    grad_qkv = mm_tn(h1, dqkv).astype(BF16)
    send_dh1 = mm_nt(after(dqkv[half:], grad_qkv[0, 0]), w_qkv).astype(BF16)
    got_dh1 = sum_to_owner(send_dh1)
    dh1_own = mm_nt(dqkv[:half], w_qkv)
    owned_rows, mark_qkv = scatter_rows(grad_qkv)
    got_dh1 = after(got_dh1, mark_qkv[0], mark_proj[1], block_out[0, 0])
    dh1 = dh1_own + got_dh1
    owned_qkv = jnp.transpose(owned_rows.reshape(-1, 3, width), (1, 0, 2))
    d_g1 = jnp.sum(dh1 * n1_own, axis=0)
    d_s1 = jnp.sum(dh1, axis=0)
    grad_input = dy1 + norm_back(dh1 * g1, n1_own, r1)

    zero_row = jnp.zeros((model,), F32)
    placed_query = lax.dynamic_update_slice_in_dim(zero_row, d_bq, rank * width, 0)
    placed_value = lax.dynamic_update_slice_in_dim(zero_row, d_bv, rank * width, 0)
    placed_up = lax.dynamic_update_slice_in_dim(
        jnp.zeros((params[10:].size,), F32), d_bu, rank * units, 0
    )
    image_params = jnp.concatenate(
        [
            jnp.stack(
                [d_g1, d_s1, placed_query, placed_value, d_bo, d_l1, d_g2, d_s2, d_bd, d_l2]
            ),
            placed_up.reshape(-1, model),
        ],
        axis=0,
    )
    rows, cols = vectors.shape
    cur = jnp.transpose(image_params.reshape(rows, model // cols, cols), (1, 0, 2))
    for stride in strides_of("tensor"):
        keep, got_p = scatter_step(cur, "tensor", stride)
        cur = keep + got_p
    for stride in strides_of("dp"):
        keep, got_p = scatter_step(cur, "dp", stride)
        cur = keep + got_p
    return (
        block_out[None],
        grad_input[None],
        cur[0],
        owned_qkv,
        owned_proj.T,
        owned_up,
        owned_down.T,
    )


def solution(mesh):
    placed = (
        P("dp", "tensor", None),
        P("dp"),
        P(None, ("dp", "tensor")),
        P(None, "dp", "tensor"),
        P("tensor", "dp"),
        P("dp", "tensor"),
        P("tensor", "dp"),
        P("dp", "tensor", None),
    )
    return jax.shard_map(
        local,
        mesh=mesh,
        in_specs=placed,
        out_specs=(
            P("dp", "tensor", None),
            P("dp", "tensor", None),
            P(None, ("dp", "tensor")),
            P(None, "dp", "tensor"),
            P("tensor", "dp"),
            P("dp", "tensor"),
            P("tensor", "dp"),
        ),
        check_vma=False,
    )
```
